32 devices in a mesh: sub: 8 (over y, x, core), front: 4 (over z).
Axes of the slice: x: 2, y: 2, z: 4, core: 2. Of those that a mesh axis runs over, the one named last changes fastest.
Arguments:
- front_inverse: bfloat16 [8, 8192, 2048], P('sub', 'front'), may hold values from -0.75 to 0.75
- coupling: bfloat16 [8, 8192, 2048], P('sub', 'front'), may hold values from -0.0234375 to 0.0234375
- free_modes: bfloat16 [8, 300, 8192], P('sub', None, 'front'), may hold values from -0.125 to 0.125
- dof_offset: int32 [8, 256], P('sub', 'front'), may hold values from 0 to 2047, as said below
- interface_id: int32 [8, 256], replicated, may hold values from 0 to 1023, as said below
Outputs:
- attachment: bfloat16 [8, 256, 8192], P('sub', None, 'front')
- flexibility: float32 [1024, 1024], P(('sub', 'front'))
The draws below stay inside these ranges and needn't reach their ends.
Inputs may be any that keep to these rules, and one draw needn't show every extreme that they name: `dof_offset`: within one substructure and one front the 64 offsets are distinct, and 0 and 2047 occur among them. `interface_id`: every value occurs exactly twice in the whole array.
All inputs are finite; a program needn't handle non-finite values.
Results may differ from the reference program's by a relative error of at most 0.02.
Values may be sent and summed in bfloat16 or wider, within the bound.
No kernel may reach another device: no remote copies, remote signals or barrier semaphores. Data moves between devices by JAX's collectives and lax.ppermute only.
A program may use at most 128 MiB of HBM per device.

```python
import jax
import jax.numpy as jnp
from jax import lax

NF = 2048
M = 300
RHS = 256
SUBS = 8
FRONTS = 4
NTOT = 8192
RJ = 64
NI = 1024
N_FRONT = 4


def draw_dof_offset(key, part):
    keys = jax.random.split(key, SUBS * FRONTS)

    def one_block(block_key):
        first_key, second_key = jax.random.split(block_key)
        inner = (jax.random.permutation(first_key, NF - 2)[:RJ - 2] + 1).astype(jnp.int32)
        values = jnp.concatenate([jnp.array([0, NF - 1], jnp.int32), inner])
        return jax.random.permutation(second_key, values)
    return jax.vmap(one_block)(keys).reshape(SUBS, RHS).astype(jnp.int32)


def draw_interface_id(key, part):
    values = jnp.arange(SUBS * RHS, dtype=jnp.int32) // 2
    return jax.random.permutation(key, values).reshape(SUBS, RHS).astype(jnp.int32)


def block_scale(own_key, dims, shards, least, top_value):
    def one(position, parts):
        draws = jax.random.uniform(jax.random.fold_in(jax.random.fold_in(own_key, 6), position), (parts,), jnp.float32, least / len(shards), top_value / len(shards))
        return jnp.repeat(jnp.exp(draws), dims[position] // parts).reshape((-1,) + (1,) * (len(dims) - position - 1))

    level = one(*shards[0])
    for cut in shards[1:]:
        level = level * one(*cut)
    return level


def bell_draw(own_key, extent, width, limit, shards=(), kind=jnp.bfloat16):
    values = jax.random.normal(own_key, extent, jnp.float32) * width
    if len(shards) > 0:
        values = block_scale(own_key, extent, shards, -0.22, 0.18) * values
    return jnp.clip(values, min=-limit, max=limit).astype(kind)


def setup_inputs(seed: int = 0) -> dict:
    arg_keys = jax.random.split(jax.random.key(seed), 6)
    return {
        "front_inverse": bell_draw(arg_keys[0], (SUBS, NTOT, NF), (NF // 32) ** -0.5, 0.75, ((0, 8), (1, 4))),
        "coupling": bell_draw(arg_keys[1], (SUBS, NTOT, NF), (32 * NF) ** -0.5, 0.0234375, ((0, 8), (1, 4))),
        "free_modes": bell_draw(arg_keys[2], (SUBS, M, NTOT), (NF * N_FRONT // 4) ** -0.5, 0.125, ((0, 8), (2, 4))),
        "dof_offset": draw_dof_offset(jax.random.fold_in(arg_keys[5], 71), 0),
        "interface_id": draw_interface_id(jax.random.fold_in(arg_keys[5], 71), 0),
    }


def contract_last(left, right):
    return lax.dot_general(left, right, (((1,), (1,)), ((), ())), preferred_element_type=jnp.float32)


def reference(front_inverse, coupling, free_modes, dof_offset, interface_id):
    column_ids = jnp.arange(RHS, dtype=jnp.int32)
    row_ids = jnp.arange(NF, dtype=jnp.int32)
    dual_ids = jnp.arange(NI, dtype=jnp.int32)
    holder = column_ids // RJ

    def per_sub(flex, index):
        inverse_all = lax.dynamic_index_in_dim(front_inverse, index, 0, keepdims=False)
        coupling_all = lax.dynamic_index_in_dim(coupling, index, 0, keepdims=False)
        modes_all = lax.dynamic_index_in_dim(free_modes, index, 0, keepdims=False)
        offsets = lax.dynamic_index_in_dim(dof_offset, index, 0, keepdims=False).astype(jnp.int32)
        labels = lax.dynamic_index_in_dim(interface_id, index, 0, keepdims=False).astype(jnp.int32)
        forward_list = []
        previous = None
        for front in range(FRONTS):
            inverse_block = inverse_all[front * NF:(front + 1) * NF]
            coupling_block = coupling_all[front * NF:(front + 1) * NF]
            load = ((holder[:, None] == front) & (offsets[:, None] == row_ids[None, :])).astype(jnp.float32)
            if previous is not None:
                load = load - contract_last(previous, coupling_block)
            solved = contract_last(load.astype(jnp.bfloat16), inverse_block).astype(jnp.bfloat16)
            forward_list.append(solved)
            previous = solved
        backward_list = [None] * FRONTS
        passed = None
        for front in range(FRONTS - 1, -1, -1):
            inverse_block = inverse_all[front * NF:(front + 1) * NF]
            coupling_block = coupling_all[front * NF:(front + 1) * NF]
            upper = forward_list[front].astype(jnp.float32)
            if passed is not None:
                upper = upper - passed.astype(jnp.float32)
            moved = jnp.dot(upper.astype(jnp.bfloat16), inverse_block, preferred_element_type=jnp.float32)
            passed = jnp.dot(moved.astype(jnp.bfloat16), coupling_block, preferred_element_type=jnp.float32).astype(jnp.bfloat16)
            backward_list[front] = moved
        displacement = jnp.concatenate(backward_list, axis=1)
        modal = contract_last(displacement.astype(jnp.bfloat16), modes_all)
        deflated = displacement - jnp.dot(modal.astype(jnp.bfloat16), modes_all, preferred_element_type=jnp.float32)
        picked = (holder * NF + offsets).astype(jnp.int32)
        block = jnp.take(deflated, picked, axis=1).T
        placed = (labels[:, None] == dual_ids[None, :]).astype(jnp.float32)
        spread = jnp.dot(block, placed, precision=lax.Precision.HIGHEST)
        flex = flex + jnp.dot(placed.T, spread, precision=lax.Precision.HIGHEST)
        return flex, deflated.astype(jnp.bfloat16)

    flex, attachment = lax.scan(per_sub, jnp.zeros((NI, NI), jnp.float32), jnp.arange(SUBS, dtype=jnp.int32))
    return attachment, flex
```

```python
import functools

import jax
import jax.numpy as jnp
from jax import lax
from jax.experimental import pallas as pl
from jax.experimental.pallas import tpu as pltpu
from jax.sharding import PartitionSpec as P

VMEM = pl.BlockSpec(memory_space=pltpu.VMEM)
SMEM = pl.BlockSpec(memory_space=pltpu.SMEM)
HBM = pl.BlockSpec(memory_space=pltpu.HBM)
GRANT = 18 << 20
BF16 = jnp.bfloat16
F32 = jnp.float32


def contract_last(left, right):
    return lax.dot_general(left, right, (((1,), (1,)), ((), ())), preferred_element_type=F32)


def tiles(total):
    width = 1024 if total % 1024 == 0 else total
    return [slice(start, start + width) for start in range(0, total, width)]


def call(body, outs, name):
    return functools.partial(
        pl.pallas_call,
        body,
        out_shape=outs,
        name=name,
        compiler_params=pltpu.CompilerParams(vmem_limit_bytes=GRANT),
    )


def hold(value):
    return pltpu.with_memory_space_constraint(value, pltpu.VMEM)


def column_of(row):
    count = row.shape[1]
    square = (count, count)
    same = lax.broadcasted_iota(jnp.int32, square, 0) == lax.broadcasted_iota(jnp.int32, square, 1)
    spread = jnp.where(same, jnp.broadcast_to(row, square).astype(F32), 0.0)
    return jnp.sum(spread, axis=1, keepdims=True).astype(jnp.int32)


def unit_rows(offsets, order):
    rows = lax.broadcasted_iota(jnp.int32, (offsets.shape[1], order), 1)
    return (rows == column_of(offsets)).astype(BF16)


def own_panel(offsets, inverse):
    count, order = offsets.shape[1], inverse.shape[0]
    cuts = tiles(order)

    def body(offsets_ref, inverse_ref, out_ref, held_ref, arrived):
        copies = [
            pltpu.make_async_copy(inverse_ref.at[cut, :], held_ref.at[cut, :], arrived.at[index])
            for index, cut in enumerate(cuts)
        ]
        for copy in copies:
            copy.start()
        pick = unit_rows(offsets_ref[...], order)
        for copy, cut in zip(copies, cuts):
            copy.wait()
            out_ref[:, cut] = contract_last(pick, held_ref[cut, :]).astype(BF16)

    outs = (jax.ShapeDtypeStruct((count, order), BF16), pltpu.VMEM(inverse.shape, BF16))
    return call(body, outs, "own_panel")(
        in_specs=[VMEM, HBM],
        out_specs=(VMEM, VMEM),
        scratch_shapes=[pltpu.SemaphoreType.DMA((len(cuts),))],
    )(offsets, inverse)


def bring(block):
    def body(block_ref, held_ref, arrived):
        copy = pltpu.make_async_copy(block_ref, held_ref, arrived)
        copy.start()
        copy.wait()

    return call(body, pltpu.VMEM(block.shape, block.dtype), "bring")(
        in_specs=[HBM],
        out_specs=VMEM,
        scratch_shapes=[pltpu.SemaphoreType.DMA],
    )(block)


def forward_step(moment, handed, coupling, inverse):
    count, order = handed.shape

    def body(handed_ref, coupling_ref, inverse_ref, out_ref, reduced_ref):
        @pl.when(lax.axis_index("front") >= moment)
        def _():
            for cut in tiles(order):
                reduced_ref[:, cut] = (-contract_last(handed_ref[...], coupling_ref[cut, :])).astype(BF16)
            for cut in tiles(order):
                out_ref[:, cut] = contract_last(reduced_ref[...], inverse_ref[cut, :]).astype(BF16)

    return call(body, jax.ShapeDtypeStruct((count, order), BF16), "forward_step")(
        in_specs=[VMEM, VMEM, VMEM],
        out_specs=VMEM,
        scratch_shapes=[pltpu.VMEM((count, order), BF16)],
    )(handed, hold(coupling), hold(inverse))


def backward_step(moment, fronts, solved, handed, coupling, inverse):
    count, order = solved[0].shape
    last = fronts - 1
    final = moment == 2 * last

    def body(*refs):
        refs = list(refs)
        solved_refs = [refs.pop(0) for _ in solved]
        handed_ref = refs.pop(0) if handed is not None else None
        coupling_ref = None if final else refs.pop(0)
        inverse_ref = refs.pop(0)
        moved_ref = refs.pop(0)
        out_ref = None if final else refs.pop(0)
        back_ref = refs.pop(0)
        front = lax.axis_index("front")
        panel = 2 * last - front - moment

        @pl.when((panel >= 0) & (panel < fronts))
        def _():
            if handed_ref is None:
                back_ref[...] = jnp.zeros_like(back_ref)
            else:
                back_ref[...] = -handed_ref[...]
            for index, ref in enumerate(solved_refs):

                @pl.when(front - panel == index)
                def _(ref=ref):
                    back_ref[...] = (back_ref[...].astype(F32) + ref[...].astype(F32)).astype(BF16)

            for cut in tiles(order):
                moved_ref[:, cut] = jnp.dot(back_ref[...], inverse_ref[:, cut], preferred_element_type=F32)
            if not final:
                back_ref[...] = moved_ref[...].astype(BF16)
                for cut in tiles(order):
                    out_ref[:, cut] = jnp.dot(
                        back_ref[...], coupling_ref[:, cut], preferred_element_type=F32
                    ).astype(BF16)

    operands = list(solved)
    if handed is not None:
        operands.append(handed)
    if not final:
        operands.append(hold(coupling))
    operands.append(hold(inverse))
    outs = [jax.ShapeDtypeStruct((count, order), F32)]
    if not final:
        outs.append(jax.ShapeDtypeStruct((count, order), BF16))
    return call(body, outs, "backward_step")(
        in_specs=[VMEM] * len(operands),
        out_specs=[VMEM] * len(outs),
        scratch_shapes=[pltpu.VMEM((count, order), BF16)],
    )(*operands)


def project(moved, modes, fronts):
    count, order = moved[0].shape
    free = modes.shape[0]
    last = fronts - 1

    def body(*refs):
        moved_refs, (modes_ref, all_ref, modal_ref, sent_ref) = refs[: len(moved)], refs[len(moved) :]
        front = lax.axis_index("front")
        for moment, ref in enumerate(moved_refs):
            panel = 2 * last - front - moment

            @pl.when((panel >= 0) & (panel < fronts))
            def _(ref=ref, panel=panel):
                all_ref[pl.ds(pl.multiple_of(panel * count, count), count), :] = ref[...]

        modal = contract_last(all_ref[...].astype(BF16), modes_ref[...])
        modal_ref[...] = modal
        sent_ref[...] = modal.astype(BF16)

    rows = fronts * count
    outs = [
        jax.ShapeDtypeStruct((rows, order), F32),
        jax.ShapeDtypeStruct((rows, free), F32),
        jax.ShapeDtypeStruct((rows, free), BF16),
    ]
    return call(body, outs, "project")(
        in_specs=[VMEM] * (len(moved) + 1), out_specs=[VMEM] * 3
    )(*moved, modes)


def add_other(value, other):
    def body(value_ref, other_ref, sum_ref, sent_ref):
        total = value_ref[...] + other_ref[...].astype(F32)
        sum_ref[...] = total
        sent_ref[...] = total.astype(BF16)

    outs = [jax.ShapeDtypeStruct(value.shape, F32), jax.ShapeDtypeStruct(value.shape, BF16)]
    return call(body, outs, "add_other")(in_specs=[VMEM] * 2, out_specs=[VMEM] * 2)(value, other)


def deflate(displacement, modal, modes, offsets):
    rows, order = displacement.shape

    def body(displacement_ref, modal_ref, modes_ref, offsets_ref, out_ref, picked_ref):
        for cut in tiles(order):
            left = jnp.dot(modal_ref[...], modes_ref[:, cut], preferred_element_type=F32)
            out_ref[:, cut] = (displacement_ref[:, cut] - left).astype(BF16)
        pick = unit_rows(offsets_ref[...], order)
        picked_ref[...] = contract_last(pick, out_ref[...]).astype(BF16)

    outs = [
        jax.ShapeDtypeStruct((rows, order), BF16),
        jax.ShapeDtypeStruct((offsets.shape[1], rows), BF16),
    ]
    return call(body, outs, "deflate")(in_specs=[VMEM] * 4, out_specs=[VMEM] * 2)(
        displacement, modal, modes, offsets
    )


def exchange_rows(value, axis):
    count = lax.axis_size(axis)
    value = value[None]
    step = 1
    while step < count:
        other = lax.ppermute(value, axis, [(i, i ^ step) for i in range(count)])
        value = jnp.concatenate([value, other])
        step *= 2
    return value


def assemble(gathered, interface_id, share):
    subs, fronts, per_front, columns = gathered.shape
    total = subs * columns // 2

    def body(gathered_ref, ids_ref, out_ref):
        sub_here, front_here = lax.axis_index("sub"), lax.axis_index("front")
        first = (sub_here * fronts + front_here) * share
        targets = first + lax.broadcasted_iota(jnp.int32, (share, columns), 0)
        holder = lax.broadcasted_iota(jnp.int32, (share, columns), 1) // per_front
        dual = lax.broadcasted_iota(jnp.int32, (total, columns), 0)
        flexibility = jnp.zeros((share, total), F32)
        for sub_step in range(subs):
            ids = ids_ref[pl.ds(sub_here ^ sub_step, 1), :]
            hit = targets == ids
            reduced = jnp.zeros((share, columns), F32)
            for front_step in range(fronts):
                front = front_here ^ front_step
                rows = hit & (holder == front)
                chosen = rows.astype(BF16)
                block = gathered_ref[sub_step, front_step]
                tall = jnp.concatenate([block] * fronts, axis=0)
                reduced = reduced + jnp.dot(chosen, tall, preferred_element_type=F32)
            place = (dual == ids).astype(BF16)
            flexibility = flexibility + contract_last(reduced.astype(BF16), place)
        out_ref[...] = flexibility

    return call(body, jax.ShapeDtypeStruct((share, total), F32), "assemble")(
        in_specs=[VMEM] * 2, out_specs=VMEM
    )(gathered, interface_id)


def on_device(front_inverse, coupling, free_modes, dof_offset, interface_id):
    inverse_block = front_inverse[0]
    coupling_block = coupling[0]
    mode_block = free_modes[0]
    subs_all, columns_all = interface_id.shape
    fronts = lax.axis_size("front")

    own, inverse_block = own_panel(dof_offset, inverse_block)
    coupling_block = bring(coupling_block)
    solved = [own]
    moved = []
    arriving = None
    last = fronts - 1
    for moment in range(2 * fronts - 1):
        if 0 < moment < fronts:
            pairs = [(i, i + 1) for i in range(moment - 1, last)]
            handed = lax.ppermute(solved[-1], "front", pairs)
            solved.append(forward_step(moment, handed, coupling_block, inverse_block))
        outcome = backward_step(moment, fronts, solved, arriving, coupling_block, inverse_block)
        moved.append(outcome[0])
        if moment < 2 * last:
            pairs = [(i, i - 1) for i in range(1, fronts) if last - moment <= i <= 2 * last - moment]
            arriving = lax.ppermute(outcome[1], "front", pairs)

    displacement, modal, sent = project(moved, mode_block, fronts)
    step = 1
    while step < fronts:
        other = lax.ppermute(sent, "front", [(i, i ^ step) for i in range(fronts)])
        modal, sent = add_other(modal, other)
        step *= 2
    deflated, own_rows = deflate(displacement, sent, mode_block, dof_offset)
    gathered = exchange_rows(exchange_rows(own_rows, "front"), "sub")
    share = subs_all * columns_all // 2 // (lax.axis_size("sub") * fronts)
    return (deflated[None], assemble(gathered, interface_id, share))


def solution(mesh):
    return jax.shard_map(
        on_device,
        mesh=mesh,
        in_specs=(
            P("sub", "front", None),
            P("sub", "front", None),
            P("sub", None, "front"),
            P("sub", "front"),
            P(),
        ),
        out_specs=(P("sub", None, "front"), P(("sub", "front"), None)),
        check_vma=False,
    )
```
